512 devices in a mesh: seg: 32 (over x, y, core), blk: 16 (over z).
Axes of the slice: x: 4, y: 4, z: 16, core: 2. Of those that a mesh axis runs over, the one named last changes fastest.
Arguments:
- spectra: bfloat16 [32, 16, 128, 4096], P('seg', 'blk'), may hold values from -6 to 6
- source_channels: int32 [16, 64], P('blk'), may hold values from 0 to 127, as said below
- pair_mask: int32 [16, 4], P('blk'), may hold values from 0 to 1, as said below
- channel_counts: int32 [16], P('blk'), may hold values from 64 to 128, as said below
Outputs:
- stacked: float32 [16, 4, 128, 1024], P('blk', None, 'seg')
The draws below stay inside these ranges and needn't reach their ends.
Inputs may be any that keep to these rules, and one draw needn't show every extreme that they name: `channel_counts`: every block has at least 64 live channels, and some block has all 128. `source_channels`: each block's 64 sources are distinct live channels of that block. `pair_mask`: slots whose offset leads past the fibre's ends are 0.
All inputs are finite; a program needn't handle non-finite values.
Results may differ from the reference program's by a relative error of at most 0.0095.
Values may be sent and summed in bfloat16 or wider, within the bound.
No kernel may reach another device: no remote copies, remote signals or barrier semaphores. Data moves between devices by JAX's collectives and lax.ppermute only.
A program may use at most 64 MiB of HBM per device.

```python
import math
import jax
import jax.numpy as jnp
from jax import lax

CH = 128
BINS = 2048
LAGS = 16
SRC = 64
REACH = 2
NBLK = 16
SEGMENTS = 32


def block_draw(key):
    base = jax.random.fold_in(key, 7)
    key_count = jax.random.fold_in(base, 1)
    key_full = jax.random.fold_in(base, 2)
    key_rank = jax.random.fold_in(base, 3)
    block_ids = jnp.arange(NBLK, dtype=jnp.int32)
    live_counts = jax.random.randint(key_count, (NBLK,), CH // 2, CH + 1, dtype=jnp.int32)
    full_block = jax.random.randint(key_full, (), 0, NBLK, dtype=jnp.int32)
    live_counts = jnp.where(block_ids == full_block, CH, live_counts)
    channel_ids = jnp.arange(CH, dtype=jnp.int32)
    priority = jax.random.randint(key_rank, (NBLK, CH), 0, 1024, dtype=jnp.int32) * CH + channel_ids[None, :]
    priority = jnp.where(channel_ids[None, :] < live_counts[:, None], priority, priority + 2048 * CH)
    ranking = jnp.argsort(priority, axis=1)
    return (live_counts.astype(jnp.int32), ranking[:, :SRC].astype(jnp.int32))


def draw_channel_counts(key, part):
    return block_draw(key)[0]


def draw_source_channels(key, part):
    return block_draw(key)[1]


def draw_pair_mask(key, part):
    coin_flips = jax.random.randint(jax.random.fold_in(key, 11), (NBLK, 2 * REACH), 0, 4, dtype=jnp.int32)
    slot_ids = jnp.arange(2 * REACH, dtype=jnp.int32)
    offsets = jnp.where(slot_ids < REACH, slot_ids - REACH, slot_ids - REACH + 1)
    target = jnp.arange(NBLK, dtype=jnp.int32)[:, None] + offsets[None, :]
    inside = jnp.logical_and(target >= 0, target < NBLK)
    return jnp.where(jnp.logical_and(coin_flips > 0, inside), 1, 0).astype(jnp.int32)


def levels(stream_key, shape, pieces, low, top_value):
    def one(position, blocks):
        steps = jax.random.uniform(jax.random.fold_in(jax.random.fold_in(stream_key, 6), position), (blocks,), jnp.float32, low / len(pieces), top_value / len(pieces))
        return jnp.repeat(jnp.exp(steps), shape[position] // blocks).reshape((-1,) + (1,) * (len(shape) - position - 1))

    factor_of = one(*pieces[0])
    for cut in pieces[1:]:
        factor_of = factor_of * one(*cut)
    return factor_of


def gaussian(own_key, shape, spread, most, shards=(), held_as=jnp.bfloat16):
    result = spread * jax.random.normal(own_key, shape, jnp.float32)
    if shards:
        result = result * levels(own_key, shape, shards, -0.22, 0.18)
    return jnp.clip(result, -most, most).astype(held_as)


def setup_inputs(seed: int = 0) -> dict:
    seeds = jax.random.split(jax.random.key(seed), 5)
    spectra = gaussian(seeds[0], (SEGMENTS, NBLK, CH, 2 * BINS), 1.0, 6.0, ((0, 32), (1, 16)))
    source_channels = draw_source_channels(jax.random.fold_in(seeds[4], 71), 0)
    pair_mask = draw_pair_mask(jax.random.fold_in(seeds[4], 71), 0)
    channel_counts = draw_channel_counts(jax.random.fold_in(seeds[4], 71), 0)
    return dict(spectra=spectra, source_channels=source_channels, pair_mask=pair_mask, channel_counts=channel_counts)


def slot_offsets():
    return [slot_index - REACH if slot_index < REACH else slot_index - REACH + 1 for slot_index in range(2 * REACH)]

def make_table(bin_count, lag_count):
    freq_index = lax.broadcasted_iota(jnp.int32, (bin_count, lag_count), 0)
    lag_index = lax.broadcasted_iota(jnp.int32, (bin_count, lag_count), 1) - lag_count // 2
    turn_count = jnp.mod(freq_index * lag_index, 2 * bin_count)
    phase_angle = turn_count.astype(jnp.float32) * (math.pi / bin_count)
    scaling = 1.0 / math.sqrt(2.0 * bin_count)
    return jnp.concatenate([jnp.cos(phase_angle) * scaling, -jnp.sin(phase_angle) * scaling], axis=0).astype(jnp.bfloat16)

def source_kernel(sources, table):
    bin_count = table.shape[0] // 2
    source_re = sources[:, :bin_count].astype(jnp.float32).T[:, :, None]
    source_im = sources[:, bin_count:].astype(jnp.float32).T[:, :, None]
    table_re = table[:bin_count].astype(jnp.float32)[:, None, :]
    table_im = table[bin_count:].astype(jnp.float32)[:, None, :]
    upper = source_re * table_re + source_im * table_im
    lower = source_im * table_re - source_re * table_im
    joined = jnp.concatenate([upper, lower], axis=0)
    return joined.reshape(2 * bin_count, -1).astype(jnp.bfloat16)

def reference(spectra, source_channels, pair_mask, channel_counts):
    lag_table = make_table(BINS, LAGS)
    channel_ids = jnp.arange(CH, dtype=jnp.int32)
    live_rows = channel_ids[None, :] < channel_counts[:, None]
    masked = jnp.where(live_rows[None, :, :, None], spectra, jnp.zeros_like(spectra))
    offsets = slot_offsets()

    def per_block(block_index):
        own_block = lax.dynamic_index_in_dim(masked, block_index, 1, keepdims=False)
        chosen = lax.dynamic_index_in_dim(source_channels, block_index, 0, keepdims=False)
        flags = lax.dynamic_index_in_dim(pair_mask, block_index, 0, keepdims=False)
        weights = []
        neighbours = []
        for slot_index, offset in enumerate(offsets):
            target = block_index + offset
            inside = jnp.logical_and(target >= 0, target < NBLK)
            neighbours.append(lax.dynamic_index_in_dim(masked, jnp.clip(target, 0, NBLK - 1).astype(jnp.int32), 1, keepdims=False))
            weights.append(jnp.where(inside, flags[slot_index], 0).astype(jnp.float32))

        def add_segment(segment, running):
            sources = jnp.take(own_block[segment], chosen, axis=0)
            kernel = source_kernel(sources, lag_table)
            terms = [jnp.dot(near[segment], kernel, preferred_element_type=jnp.float32) * weight for near, weight in zip(neighbours, weights)]
            return running + jnp.stack(terms)
        return lax.fori_loop(0, SEGMENTS, add_segment, jnp.zeros((2 * REACH, CH, SRC * LAGS), jnp.float32))
    stacked = lax.map(per_block, jnp.arange(NBLK, dtype=jnp.int32))
    return stacked * (1.0 / math.sqrt(SEGMENTS))
```

```python
import math

import jax
import jax.numpy as jnp
from jax import lax
from jax.sharding import PartitionSpec as P

LAGS = 16


def passed_along(value, axis, by):
    devices = lax.axis_size(axis)
    pairs = [(i, i + by) for i in range(devices) if 0 <= i + by < devices]
    return lax.ppermute(value, axis, pairs)


def make_table(bin_count, lag_count):
    freq_index = lax.broadcasted_iota(jnp.int32, (bin_count, lag_count), 0)
    lag_index = lax.broadcasted_iota(jnp.int32, (bin_count, lag_count), 1) - lag_count // 2
    turn_count = jnp.mod(freq_index * lag_index, 2 * bin_count)
    phase_angle = turn_count.astype(jnp.float32) * (math.pi / bin_count)
    scaling = 1.0 / math.sqrt(2.0 * bin_count)
    return jnp.concatenate(
        [jnp.cos(phase_angle) * scaling, -jnp.sin(phase_angle) * scaling], axis=0
    ).astype(jnp.bfloat16)


def source_kernel(sources, table):
    bin_count = table.shape[0] // 2
    source_re = sources[:, :bin_count].astype(jnp.float32).T[:, :, None]
    source_im = sources[:, bin_count:].astype(jnp.float32).T[:, :, None]
    table_re = table[:bin_count].astype(jnp.float32)[:, None, :]
    table_im = table[bin_count:].astype(jnp.float32)[:, None, :]
    upper = source_re * table_re + source_im * table_im
    lower = source_im * table_re - source_re * table_im
    joined = jnp.concatenate([upper, lower], axis=0)
    return joined.reshape(2 * bin_count, -1).astype(jnp.bfloat16)


def local(spectra, source_channels, pair_mask, channel_counts):
    own_block = spectra[0, 0]
    channels = own_block.shape[0]
    bin_count = own_block.shape[1] // 2
    segments = lax.axis_size("seg")
    rows = channels // segments
    lag_table = make_table(bin_count, LAGS)
    live_rows = lax.broadcasted_iota(jnp.int32, (channels, 1), 0) < channel_counts[0]
    own_block = jnp.where(live_rows, own_block, jnp.zeros_like(own_block))
    above = passed_along(own_block, "blk", -1)
    below = passed_along(own_block, "blk", 1)
    chosen = source_channels[0]
    chosen_above = passed_along(chosen, "blk", -1)
    chosen_below = passed_along(chosen, "blk", 1)

    def kernel_of(block, channel):
        return source_kernel(jnp.take(block, channel, axis=0), lag_table)

    def product(block, kernel):
        return jnp.dot(block, kernel, preferred_element_type=jnp.float32).astype(jnp.bfloat16)

    own_kernel = kernel_of(own_block, chosen)
    terms = jnp.stack([
        product(below, kernel_of(above, chosen_above)),
        product(below, own_kernel),
        product(above, own_kernel),
        product(above, kernel_of(below, chosen_below)),
    ])
    columns = terms.shape[-1]
    pieces = terms.reshape(4, segments, rows, columns).transpose(1, 0, 2, 3)
    pieces = pieces.reshape(segments, 4 * rows, columns)
    received = lax.all_to_all(pieces, "seg", 0, 0, tiled=True)
    summed = jnp.sum(received.astype(jnp.float32), axis=0).reshape(4, rows, columns)
    moved_up = passed_along(summed[0], "blk", 1)
    moved_down = passed_along(summed[3], "blk", -1)
    joined = jnp.stack([moved_up, summed[1], summed[2], moved_down])
    weights = pair_mask[0].astype(jnp.float32) * (1.0 / math.sqrt(segments))
    return (joined * weights[:, None, None])[None]


def solution(mesh):
    in_specs = (P("seg", "blk", None, None), P("blk", None), P("blk", None), P("blk"))
    out_specs = P("blk", None, "seg", None)
    return jax.shard_map(local, mesh=mesh, in_specs=in_specs, out_specs=out_specs, check_vma=False)
```

```python
import functools
import math

import jax
import jax.numpy as jnp
from jax import lax
from jax.experimental import pallas as pl
from jax.experimental.pallas import tpu as pltpu
from jax.sharding import PartitionSpec as P

LAGS = 16
CHUNKS = 2
TILE = 512
NT = (((1,), (1,)), ((), ()))


def passed_along(value, axis, by):
    devices = lax.axis_size(axis)
    pairs = [(i, i + by) for i in range(devices) if 0 <= i + by < devices]
    return lax.ppermute(value, axis, pairs)


def make_table(bin_count, lag_count):
    freq_index = lax.broadcasted_iota(jnp.int32, (lag_count, bin_count), 1)
    lag_index = lax.broadcasted_iota(jnp.int32, (lag_count, bin_count), 0) - lag_count // 2
    turn_count = jnp.mod(freq_index * lag_index, 2 * bin_count)
    phase_angle = turn_count.astype(jnp.float32) * (math.pi / bin_count)
    scaling = 1.0 / math.sqrt(2.0 * bin_count)
    return jnp.stack(
        [jnp.cos(phase_angle) * scaling, -jnp.sin(phase_angle) * scaling]
    ).astype(jnp.bfloat16)


def products_kernel(first, last, *refs):
    refs = list(refs)
    hot_above, hot_below, table, own, above, below = refs[:6]
    before = None if first else refs[6]
    out = refs[6 if first else 7]
    source_ref, kernel_ref, pair_ref = refs[-4:-1] if last else refs[-3:]
    sums = refs[-1] if last else out
    channels, half = own.shape[0], own.shape[1] // 2
    source_count, lag_count = hot_above.shape[0], table.shape[0]
    per = TILE // lag_count
    table_re = table[:, :half].astype(jnp.float32)
    table_im = table[:, half:].astype(jnp.float32)
    sides = ((hot_above, above, (below, own)), (hot_below, below, (own, above)))
    for side, (hot, near, pair) in enumerate(sides):
        source_ref[...] = jnp.dot(hot[...], near[...], preferred_element_type=jnp.float32)
        pair_ref[:channels, :] = pair[0][...]
        pair_ref[channels:, :] = pair[1][...]

        @pl.loop(0, source_count // per)
        def _(step):
            for place in range(per):
                source = step * per + place
                rows = slice(place * lag_count, (place + 1) * lag_count)
                source_re = source_ref[pl.ds(source, 1), :half]
                source_im = source_ref[pl.ds(source, 1), half:]
                upper = source_re * table_re + source_im * table_im
                lower = source_im * table_re - source_re * table_im
                kernel_ref[rows, :half] = upper.astype(jnp.bfloat16)
                kernel_ref[rows, half:] = lower.astype(jnp.bfloat16)
            rows = pl.ds(pl.multiple_of(step * TILE, TILE), TILE)
            term = lax.dot_general(
                kernel_ref[...], pair_ref[...], NT, preferred_element_type=jnp.float32
            )
            if not first:
                term = term + before[side, rows, :]
            sums[side, rows, :] = term.astype(sums.dtype)

    if last:
        segments, rows = out.shape[0], out.shape[1] // 4
        size = 2 * channels
        to = lax.broadcasted_iota(jnp.int32, (size, size), 0)
        frm = lax.broadcasted_iota(jnp.int32, (size, size), 1)
        wanted = (to // rows % 2) * channels + to // (2 * rows) * rows + to % rows
        order = (frm == wanted).astype(jnp.float32).astype(jnp.bfloat16)
        for start in range(0, source_count * lag_count, 256):
            part = slice(start, start + 256)
            halves = [
                lax.dot_general(
                    order, sums[side, part, :], NT, preferred_element_type=jnp.float32
                ).reshape(segments, 2 * rows, 256)
                for side in range(2)
            ]
            out[:, :, part] = jnp.concatenate(halves, axis=1).astype(jnp.bfloat16)


def products(hots, table, own, above, below, before, last, segments):
    channels, width = own.shape
    source_count, lag_count = hots[0].shape[0], table.shape[0]
    columns = source_count * lag_count
    first = before is None
    scratch = [
        pltpu.VMEM((source_count, width), jnp.float32),
        pltpu.VMEM((TILE, width), jnp.bfloat16),
        pltpu.VMEM((2 * channels, width), jnp.bfloat16),
    ]
    if last:
        scratch.append(pltpu.VMEM((2, columns, 2 * channels), jnp.bfloat16))
        shape = jax.ShapeDtypeStruct((segments, 4 * channels // segments, columns), jnp.bfloat16)
    else:
        shape = jax.ShapeDtypeStruct((2, columns, 2 * channels), jnp.float32)
    operands = (*hots, table, own, above, below) + (() if first else (before,))
    return pl.pallas_call(
        functools.partial(products_kernel, first, last),
        out_shape=shape,
        in_specs=[pl.BlockSpec(memory_space=pltpu.VMEM)] * len(operands),
        out_specs=pl.BlockSpec(memory_space=pltpu.VMEM),
        scratch_shapes=scratch,
        cost_estimate=pl.CostEstimate(
            flops=8 * columns * channels * width, bytes_accessed=6 * channels * width, transcendentals=0
        ),
        compiler_params=pltpu.CompilerParams(vmem_limit_bytes=32 << 20),
    )(*operands)


def local(spectra, source_channels, pair_mask, channel_counts):
    block = spectra[0, 0]
    channels, bin_count = block.shape[0], block.shape[1] // 2
    segments = lax.axis_size("seg")
    rows = channels // segments
    live_rows = lax.broadcasted_iota(jnp.int32, (channels, 1), 0) < channel_counts[0]
    part = bin_count // CHUNKS

    def chunk_of(array, index):
        re = array[..., index * part : (index + 1) * part]
        im = array[..., bin_count + index * part : bin_count + (index + 1) * part]
        return jnp.concatenate([re, im], axis=-1)

    own, above, below = [], [], []
    for index in range(CHUNKS):
        piece = chunk_of(block, index)
        piece = jnp.where(live_rows, piece, jnp.zeros_like(piece))
        own.append(piece)
        above.append(passed_along(piece, "blk", -1))
        below.append(passed_along(piece, "blk", 1))
    chosen = source_channels[0]
    channel_ids = lax.broadcasted_iota(jnp.int32, (chosen.shape[0], channels), 1)
    hots = [
        (passed_along(chosen, "blk", by)[:, None] == channel_ids).astype(jnp.bfloat16)
        for by in (-1, 1)
    ]
    table = make_table(bin_count, LAGS)
    table = jnp.concatenate([table[0], table[1]], axis=-1)
    sums = None
    for index in range(CHUNKS):
        sums = products(
            hots, chunk_of(table, index), own[index], above[index], below[index], sums, index == CHUNKS - 1, segments
        )
    received = lax.all_to_all(sums, "seg", 0, 0, tiled=True)
    summed = jnp.sum(received.astype(jnp.float32), axis=0)
    from_below = passed_along(summed[: 2 * rows], "blk", 1)
    from_above = passed_along(summed[2 * rows :], "blk", -1)
    joined = jnp.concatenate([from_below, from_above], axis=0).reshape(4, rows, -1)
    weights = pair_mask[0].astype(jnp.float32) * (1.0 / math.sqrt(segments))
    return (joined * weights[:, None, None])[None]


def solution(mesh):
    in_specs = (P("seg", "blk", None, None), P("blk", None), P("blk", None), P("blk"))
    out_specs = P("blk", None, "seg", None)
    return jax.shard_map(local, mesh=mesh, in_specs=in_specs, out_specs=out_specs, check_vma=False)
```

```python
import functools
import math

import jax
import jax.numpy as jnp
from jax import lax
from jax.experimental import pallas as pl
from jax.experimental.pallas import tpu as pltpu
from jax.sharding import PartitionSpec as P

LAGS = 16
CHUNKS = (5, 3)
TILE = 512
TAG = 128
NT = (((1,), (1,)), ((), ()))
TN = (((0,), (0,)), ((), ()))


def passed_along(value, by):
    segments, blocks = lax.axis_size("seg"), lax.axis_size("blk")
    pairs = []
    for segment in range(segments):
        step = by if segment % 2 == 0 else -by
        for block in range(blocks):
            if 0 <= block + step < blocks:
                pairs.append((segment * blocks + block, segment * blocks + block + step))
    return lax.ppermute(value, ("seg", "blk"), pairs)


def to_other_core(value):
    return lax.ppermute(value, "seg", [(i, i ^ 1) for i in range(lax.axis_size("seg"))])


def make_table(bin_count, lag_count):
    freq_index = lax.broadcasted_iota(jnp.int32, (lag_count, bin_count), 1)
    lag_index = lax.broadcasted_iota(jnp.int32, (lag_count, bin_count), 0) - lag_count // 2
    turn_count = jnp.mod(freq_index * lag_index, 2 * bin_count)
    phase_angle = turn_count.astype(jnp.float32) * (math.pi / bin_count)
    scaling = 1.0 / math.sqrt(2.0 * bin_count)
    return jnp.stack(
        [jnp.cos(phase_angle) * scaling, -jnp.sin(phase_angle) * scaling]
    ).astype(jnp.bfloat16)


def products_kernel(first, last, *refs):
    refs = list(refs)
    tag, table, own, near, far = refs[:5]
    before = None if first else refs[5]
    out = refs[5 if first else 6]
    source_ref, kernel_ref, pair_ref = refs[-4:-1] if last else refs[-3:]
    sums = refs[-1] if last else out
    channels, half = own.shape[0], table.shape[1] // 2
    source_count, lag_count = source_ref.shape[0], table.shape[0]
    per = TILE // lag_count
    table_re = table[:, :half].astype(jnp.float32)
    table_im = table[:, half:].astype(jnp.float32)
    hot = tag[:, tag.shape[1] - TAG :]
    picked = lax.dot_general(hot, near[:, : 2 * half], TN, preferred_element_type=jnp.float32)
    source_ref[...] = picked[:source_count]
    pair_ref[:channels, :] = far[:, : 2 * half]
    pair_ref[channels:, :] = own[:, : 2 * half]

    @pl.loop(0, source_count // per)
    def _(step):
        for place in range(per):
            source = step * per + place
            rows = slice(place * lag_count, (place + 1) * lag_count)
            source_re = source_ref[pl.ds(source, 1), :half]
            source_im = source_ref[pl.ds(source, 1), half:]
            upper = source_re * table_re + source_im * table_im
            lower = source_im * table_re - source_re * table_im
            kernel_ref[rows, :half] = upper.astype(jnp.bfloat16)
            kernel_ref[rows, half:] = lower.astype(jnp.bfloat16)
        rows = pl.ds(pl.multiple_of(step * TILE, TILE), TILE)
        term = lax.dot_general(
            kernel_ref[...], pair_ref[...], NT, preferred_element_type=jnp.float32
        )
        if not first:
            term = term + before[rows, :]
        sums[rows, :] = term.astype(sums.dtype)

    if last:
        chips, rows = out.shape[0], out.shape[1] // 2
        size = 2 * channels
        to = lax.broadcasted_iota(jnp.int32, (size, size), 0)
        frm = lax.broadcasted_iota(jnp.int32, (size, size), 1)
        wanted = to // rows % 2 * channels + to // (2 * rows) * rows + to % rows
        order = (frm == wanted).astype(jnp.float32).astype(jnp.bfloat16)
        for start in range(0, source_count * lag_count, 256):
            part = slice(start, start + 256)
            turned = lax.dot_general(order, sums[part, :], NT, preferred_element_type=jnp.float32)
            out[:, :, part] = turned.reshape(chips, 2 * rows, 256).astype(jnp.bfloat16)


def products(tag, source_count, table, own, near, far, before, last, chips):
    channels, (lag_count, width) = own.shape[0], table.shape
    columns = source_count * lag_count
    first = before is None
    scratch = [
        pltpu.VMEM((source_count, width), jnp.float32),
        pltpu.VMEM((TILE, width), jnp.bfloat16),
        pltpu.VMEM((2 * channels, width), jnp.bfloat16),
    ]
    if last:
        scratch.append(pltpu.VMEM((columns, 2 * channels), jnp.bfloat16))
        shape = jax.ShapeDtypeStruct((chips, 2 * channels // chips, columns), jnp.bfloat16)
    else:
        shape = jax.ShapeDtypeStruct((columns, 2 * channels), jnp.float32)
    operands = (tag, table, own, near, far) + (() if first else (before,))
    return pl.pallas_call(
        functools.partial(products_kernel, first, last),
        out_shape=shape,
        in_specs=[pl.BlockSpec(memory_space=pltpu.VMEM)] * len(operands),
        out_specs=pl.BlockSpec(memory_space=pltpu.VMEM),
        scratch_shapes=scratch,
        cost_estimate=pl.CostEstimate(
            flops=4 * columns * channels * width, bytes_accessed=6 * channels * width, transcendentals=0
        ),
        compiler_params=pltpu.CompilerParams(vmem_limit_bytes=24 << 20),
    )(*operands)


def local(spectra, source_channels, pair_mask, channel_counts):
    block = spectra[0, 0]
    channels, bin_count = block.shape[0], block.shape[1] // 2
    segments = lax.axis_size("seg")
    chips, rows = segments // 2, channels // segments
    live_rows = lax.broadcasted_iota(jnp.int32, (channels, 1), 0) < channel_counts[0]
    parts = [bin_count * share // sum(CHUNKS) for share in CHUNKS]
    starts = [sum(parts[:index]) for index in range(len(parts))]

    def chunk_of(array, index):
        bins = slice(starts[index], starts[index] + parts[index])
        re, im = array[..., :bin_count], array[..., bin_count:]
        return jnp.concatenate([re[..., bins], im[..., bins]], axis=-1)

    chosen = jnp.pad(source_channels[0], (0, TAG - source_channels.shape[1]), constant_values=channels)
    channel_ids = lax.broadcasted_iota(jnp.int32, (channels, TAG), 0)
    hot = jnp.logical_and(chosen[None, :] == channel_ids, live_rows).astype(jnp.bfloat16)
    own, one, other = [], [], []
    for index in range(len(parts)):
        piece = chunk_of(block, index)
        piece = jnp.where(live_rows, piece, jnp.zeros_like(piece))
        if index == 0:
            piece = jnp.concatenate([piece, hot], axis=1)
        own.append(piece)
        one.append(passed_along(piece, 1))
        other.append(passed_along(piece, -1))
        block, _ = lax.optimization_barrier((block, piece))
    table = make_table(bin_count, LAGS)
    table = jnp.concatenate([table[0], table[1]], axis=-1)
    sources = source_channels.shape[1]

    def side(near, far, sums, index):
        last = index == len(parts) - 1
        return products(
            near[0], sources, chunk_of(table, index), own[index], near[index], far[index], sums, last, chips
        )

    given, kept = None, None
    for index in range(len(parts)):
        given = side(other, one, given, index)
        kept = side(one, other, kept, index)
        if index < len(parts) - 1:
            given, kept = lax.optimization_barrier((given, kept))
    taken = to_other_core(given)
    both = (kept.astype(jnp.float32) + taken.astype(jnp.float32)).astype(jnp.bfloat16)
    groups = [list(range(start, segments, 2)) for start in range(2)]
    received = lax.all_to_all(both, "seg", 0, 0, axis_index_groups=groups, tiled=True)
    summed = jnp.sum(received.astype(jnp.float32), axis=0)
    arrived = passed_along(summed, -1).reshape(2, 2, rows, -1)
    first_core = lax.axis_index("seg") % 2 == 0
    mine = jnp.where(first_core, arrived[:, 0], arrived[:, 1])
    theirs = to_other_core(jnp.where(first_core, arrived[:, 1], arrived[:, 0]))
    lower = jnp.where(first_core, theirs, mine)
    upper = jnp.where(first_core, mine, theirs)
    joined = jnp.concatenate([lower, upper[::-1]], axis=0)
    weights = pair_mask[0].astype(jnp.float32) * (1.0 / math.sqrt(segments))
    return (joined * weights[:, None, None])[None]


def solution(mesh):
    in_specs = (P("seg", "blk", None, None), P("blk", None), P("blk", None), P("blk"))
    out_specs = P("blk", None, "seg", None)
    return jax.shard_map(local, mesh=mesh, in_specs=in_specs, out_specs=out_specs, check_vma=False)
```

```python
import functools
import math

import jax
import jax.numpy as jnp
from jax import lax
from jax.experimental import pallas as pl
from jax.experimental.pallas import tpu as pltpu
from jax.sharding import PartitionSpec as P

LAGS = 16
CHUNKS = (5, 3)
TILE = 256
TAG = 128
NT = (((1,), (1,)), ((), ()))
TN = (((0,), (0,)), ((), ()))


def passed_along(value, by):
    segments, blocks = lax.axis_size("seg"), lax.axis_size("blk")
    pairs = []
    for segment in range(segments):
        step = by if segment % 2 == 0 else -by
        for block in range(blocks):
            if 0 <= block + step < blocks:
                pairs.append((segment * blocks + block, segment * blocks + block + step))
    return lax.ppermute(value, ("seg", "blk"), pairs)


def to_other_core(value):
    return lax.ppermute(value, "seg", [(i, i ^ 1) for i in range(lax.axis_size("seg"))])


def make_table(bin_count, lag_count):
    freq_index = lax.broadcasted_iota(jnp.int32, (lag_count, bin_count), 1)
    lag_index = lax.broadcasted_iota(jnp.int32, (lag_count, bin_count), 0) - lag_count // 2
    turn_count = jnp.mod(freq_index * lag_index, 2 * bin_count)
    phase_angle = turn_count.astype(jnp.float32) * (math.pi / bin_count)
    scaling = 1.0 / math.sqrt(2.0 * bin_count)
    return jnp.stack(
        [jnp.cos(phase_angle) * scaling, -jnp.sin(phase_angle) * scaling]
    ).astype(jnp.bfloat16)


def products_kernel(first, last, *refs):
    refs = list(refs)
    tag, table, own, near, far = refs[:5]
    before = None if first else refs[5]
    out = refs[5 if first else 6]
    source_ref, kernel_ref, pair_ref = refs[-3:]
    channels, half = own.shape[0], table.shape[1] // 2
    source_count, lag_count = source_ref.shape[0], table.shape[0]
    per = TILE // lag_count
    table_re = table[:, :half].astype(jnp.float32)
    table_im = table[:, half:].astype(jnp.float32)
    hot = tag[:, tag.shape[1] - TAG :]
    picked = lax.dot_general(hot, near[:, : 2 * half], TN, preferred_element_type=jnp.float32)
    source_ref[...] = picked[:source_count]
    pair_ref[:channels, :] = far[:, : 2 * half]
    pair_ref[channels:, :] = own[:, : 2 * half]

    def build(step):
        for place in range(per):
            source = step * per + place
            rows = slice(place * lag_count, (place + 1) * lag_count)
            source_re = source_ref[pl.ds(source, 1), :half]
            source_im = source_ref[pl.ds(source, 1), half:]
            upper = source_re * table_re + source_im * table_im
            lower = source_im * table_re - source_re * table_im
            kernel_ref[step % 2, rows, :half] = upper.astype(jnp.bfloat16)
            kernel_ref[step % 2, rows, half:] = lower.astype(jnp.bfloat16)

    def multiply(step):
        rows = slice(step * TILE, (step + 1) * TILE)
        term = lax.dot_general(
            kernel_ref[step % 2], pair_ref[...], NT, preferred_element_type=jnp.float32
        )
        if not first:
            term = term + before[rows, :]
        if last:
            chips, each = out.shape[0], out.shape[1] // 2
            turned = term.T.reshape(2, chips, each, TILE)
            out[:, :, rows] = jnp.concatenate([turned[0], turned[1]], axis=1).astype(jnp.bfloat16)
        else:
            out[rows, :] = term

    steps = source_count // per
    build(0)
    for step in range(1, steps):
        build(step)
        multiply(step - 1)
    multiply(steps - 1)


def products(tag, source_count, table, own, near, far, before, last, chips):
    channels, (lag_count, width) = own.shape[0], table.shape
    columns = source_count * lag_count
    first = before is None
    scratch = [
        pltpu.VMEM((source_count, width), jnp.float32),
        pltpu.VMEM((2, TILE, width), jnp.bfloat16),
        pltpu.VMEM((2 * channels, width), jnp.bfloat16),
    ]
    if last:
        shape = jax.ShapeDtypeStruct((chips, 2 * channels // chips, columns), jnp.bfloat16)
    else:
        shape = jax.ShapeDtypeStruct((columns, 2 * channels), jnp.float32)
    operands = (tag, table, own, near, far) + (() if first else (before,))
    return pl.pallas_call(
        functools.partial(products_kernel, first, last),
        out_shape=shape,
        in_specs=[pl.BlockSpec(memory_space=pltpu.VMEM)] * len(operands),
        out_specs=pl.BlockSpec(memory_space=pltpu.VMEM),
        scratch_shapes=scratch,
        cost_estimate=pl.CostEstimate(
            flops=4 * columns * channels * width, bytes_accessed=6 * channels * width, transcendentals=0
        ),
        compiler_params=pltpu.CompilerParams(vmem_limit_bytes=24 << 20),
    )(*operands)


def local(spectra, source_channels, pair_mask, channel_counts):
    block = spectra[0, 0]
    channels, bin_count = block.shape[0], block.shape[1] // 2
    segments = lax.axis_size("seg")
    chips, rows = segments // 2, channels // segments
    live_rows = lax.broadcasted_iota(jnp.int32, (channels, 1), 0) < channel_counts[0]
    parts = [bin_count * share // sum(CHUNKS) for share in CHUNKS]
    starts = [sum(parts[:index]) for index in range(len(parts))]

    def chunk_of(array, index):
        bins = slice(starts[index], starts[index] + parts[index])
        re, im = array[..., :bin_count], array[..., bin_count:]
        return jnp.concatenate([re[..., bins], im[..., bins]], axis=-1)

    sources = source_channels.shape[1]
    channel_ids = lax.broadcasted_iota(jnp.int32, (channels, sources), 0)
    hot = jnp.logical_and(source_channels == channel_ids, live_rows).astype(jnp.bfloat16)
    hot = jnp.concatenate([hot, jnp.zeros((channels, TAG - sources), jnp.bfloat16)], axis=1)
    own, one, other = [], [], []
    for index in range(len(parts)):
        piece = chunk_of(block, index)
        piece = jnp.where(live_rows, piece, jnp.zeros_like(piece))
        if index == 0:
            piece = jnp.concatenate([piece, hot], axis=1)
        own.append(piece)
        one.append(passed_along(piece, 1))
        other.append(passed_along(piece, -1))
        block, _ = lax.optimization_barrier((block, piece))
    table = make_table(bin_count, LAGS)
    table = jnp.concatenate([table[0], table[1]], axis=-1)
    def side(near, far, sums, index):
        last = index == len(parts) - 1
        return products(
            near[0], sources, chunk_of(table, index), own[index], near[index], far[index], sums, last, chips
        )

    given, kept = None, None
    for index in range(len(parts)):
        given = side(other, one, given, index)
        kept = side(one, other, kept, index)
        if index < len(parts) - 1:
            given, kept = lax.optimization_barrier((given, kept))
    taken = to_other_core(given)
    both = (kept.astype(jnp.float32) + taken.astype(jnp.float32)).astype(jnp.bfloat16)
    groups = [list(range(start, segments, 2)) for start in range(2)]
    received = lax.all_to_all(both, "seg", 0, 0, axis_index_groups=groups, tiled=True)
    summed = jnp.sum(received.astype(jnp.float32), axis=0)
    arrived = passed_along(summed, -1).reshape(2, 2, rows, -1)
    first_core = lax.axis_index("seg") % 2 == 0
    mine = jnp.where(first_core, arrived[:, 0], arrived[:, 1])
    theirs = to_other_core(jnp.where(first_core, arrived[:, 1], arrived[:, 0]))
    lower = jnp.where(first_core, theirs, mine)
    upper = jnp.where(first_core, mine, theirs)
    joined = jnp.concatenate([lower, upper[::-1]], axis=0)
    weights = pair_mask[0].astype(jnp.float32) * (1.0 / math.sqrt(segments))
    return (joined * weights[:, None, None])[None]


def solution(mesh):
    in_specs = (P("seg", "blk", None, None), P("blk", None), P("blk", None), P("blk"))
    out_specs = P("blk", None, "seg", None)
    return jax.shard_map(local, mesh=mesh, in_specs=in_specs, out_specs=out_specs, check_vma=False)
```

```python
import functools
import math

import jax
import jax.numpy as jnp
from jax import lax
from jax.experimental import pallas as pl
from jax.experimental.pallas import tpu as pltpu
from jax.sharding import PartitionSpec as P

LAGS = 16
CHUNKS = (5, 3)
TILE = 256
TAG = 128
NT = (((1,), (1,)), ((), ()))
TN = (((0,), (0,)), ((), ()))


def passed_along(value, by):
    segments, blocks = lax.axis_size("seg"), lax.axis_size("blk")
    pairs = []
    for segment in range(segments):
        step = by if segment % 2 == 0 else -by
        for block in range(blocks):
            if 0 <= block + step < blocks:
                pairs.append((segment * blocks + block, segment * blocks + block + step))
    return lax.ppermute(value, ("seg", "blk"), pairs)


def to_other_core(value):
    return lax.ppermute(value, "seg", [(i, i ^ 1) for i in range(lax.axis_size("seg"))])


def make_table(bin_count, lag_count):
    freq_index = lax.broadcasted_iota(jnp.int32, (lag_count, bin_count), 1)
    lag_index = lax.broadcasted_iota(jnp.int32, (lag_count, bin_count), 0) - lag_count // 2
    turn_count = jnp.mod(freq_index * lag_index, 2 * bin_count)
    phase_angle = turn_count.astype(jnp.float32) * (math.pi / bin_count)
    scaling = 1.0 / math.sqrt(2.0 * bin_count)
    return jnp.stack(
        [jnp.cos(phase_angle) * scaling, -jnp.sin(phase_angle) * scaling]
    ).astype(jnp.bfloat16)


def products_kernel(first, last, *refs):
    refs = list(refs)
    tag, table, own, near, far = refs[:5]
    before = None if first else refs[5]
    out = refs[5 if first else 6]
    source_ref, kernel_ref, pair_ref = refs[-3:]
    channels, half = own.shape[0], table.shape[1] // 2
    source_count, lag_count = source_ref.shape[0], table.shape[0]
    per = TILE // lag_count
    table_re = table[:, :half].astype(jnp.float32)
    table_im = table[:, half:].astype(jnp.float32)
    hot = tag[:, tag.shape[1] - TAG :]
    picked = lax.dot_general(hot, near[:, : 2 * half], TN, preferred_element_type=jnp.float32)
    source_ref[...] = picked[:source_count]
    pair_ref[:channels, :] = far[:, : 2 * half]
    pair_ref[channels:, :] = own[:, : 2 * half]

    def build(step):
        for place in range(per):
            source = step * per + place
            rows = slice(place * lag_count, (place + 1) * lag_count)
            source_re = source_ref[pl.ds(source, 1), :half]
            source_im = source_ref[pl.ds(source, 1), half:]
            upper = source_re * table_re + source_im * table_im
            lower = source_im * table_re - source_re * table_im
            kernel_ref[step % 2, rows, :half] = upper.astype(jnp.bfloat16)
            kernel_ref[step % 2, rows, half:] = lower.astype(jnp.bfloat16)

    def multiply(step):
        rows = slice(step * TILE, (step + 1) * TILE)
        term = lax.dot_general(
            kernel_ref[step % 2], pair_ref[...], NT, preferred_element_type=jnp.float32
        )
        if not first:
            term = term + before[rows, :]
        if last:
            chips, each = out.shape[0], out.shape[1] // 2
            turned = term.T.reshape(2, chips, each, TILE)
            out[:, :, rows] = jnp.concatenate([turned[0], turned[1]], axis=1).astype(jnp.bfloat16)
        else:
            out[rows, :] = term

    steps = source_count // per
    build(0)
    for step in range(1, steps):
        build(step)
        multiply(step - 1)
    multiply(steps - 1)


def pack_kernel(count, chosen_ref, block_ref, *refs):
    *outs, chosen, block, chosen_sem, block_sem = refs
    copies = (
        pltpu.make_async_copy(block_ref, block, block_sem),
        pltpu.make_async_copy(chosen_ref, chosen, chosen_sem),
    )
    for copy in copies:
        copy.start()
    for copy in copies:
        copy.wait()
    channels, bin_count = block.shape[0], block.shape[1] // 2
    start = 0
    for index, out in enumerate(outs):
        bins = (out.shape[1] - (TAG if index == 0 else 0)) // 2
        live = lax.broadcasted_iota(jnp.int32, (channels, bins), 0) < count[0]
        for half in range(2):
            part = block[:, half * bin_count + start : half * bin_count + start + bins]
            part = jnp.where(live, part.astype(jnp.float32), 0.0).astype(jnp.bfloat16)
            out[:, half * bins : (half + 1) * bins] = part
        start += bins
    tag = outs[0].shape[1] - TAG
    sources = chosen.shape[1]
    rows = lax.broadcasted_iota(jnp.int32, (channels, sources), 0)
    hot = jnp.logical_and(chosen[...] == rows, rows < count[0])
    outs[0][:, tag:] = jnp.zeros((channels, TAG), jnp.bfloat16)
    outs[0][:, tag : tag + sources] = jnp.where(hot, 1.0, 0.0).astype(jnp.bfloat16)


def products(tag, source_count, table, own, near, far, before, last, chips):
    channels, (lag_count, width) = own.shape[0], table.shape
    columns = source_count * lag_count
    first = before is None
    scratch = [
        pltpu.VMEM((source_count, width), jnp.float32),
        pltpu.VMEM((2, TILE, width), jnp.bfloat16),
        pltpu.VMEM((2 * channels, width), jnp.bfloat16),
    ]
    if last:
        shape = jax.ShapeDtypeStruct((chips, 2 * channels // chips, columns), jnp.bfloat16)
    else:
        shape = jax.ShapeDtypeStruct((columns, 2 * channels), jnp.float32)
    operands = (tag, table, own, near, far) + (() if first else (before,))
    return pl.pallas_call(
        functools.partial(products_kernel, first, last),
        out_shape=shape,
        in_specs=[pl.BlockSpec(memory_space=pltpu.VMEM)] * len(operands),
        out_specs=pl.BlockSpec(memory_space=pltpu.VMEM),
        scratch_shapes=scratch,
        cost_estimate=pl.CostEstimate(
            flops=4 * columns * channels * width, bytes_accessed=6 * channels * width, transcendentals=0
        ),
        compiler_params=pltpu.CompilerParams(vmem_limit_bytes=24 << 20),
    )(*operands)


def local(spectra, source_channels, pair_mask, channel_counts):
    block = spectra[0, 0]
    channels, bin_count = block.shape[0], block.shape[1] // 2
    segments = lax.axis_size("seg")
    chips, rows = segments // 2, channels // segments
    parts = [bin_count * share // sum(CHUNKS) for share in CHUNKS]
    starts = [sum(parts[:index]) for index in range(len(parts))]

    def chunk_of(array, index):
        bins = slice(starts[index], starts[index] + parts[index])
        re, im = array[..., :bin_count], array[..., bin_count:]
        return jnp.concatenate([re[..., bins], im[..., bins]], axis=-1)

    sources = source_channels.shape[1]
    vmem = pl.BlockSpec(memory_space=pltpu.VMEM)
    own = pl.pallas_call(
        pack_kernel,
        out_shape=[
            jax.ShapeDtypeStruct((channels, 2 * bins + (0 if index else TAG)), jnp.bfloat16)
            for index, bins in enumerate(parts)
        ],
        in_specs=[pl.BlockSpec(memory_space=pltpu.SMEM)] + [pl.BlockSpec(memory_space=pltpu.HBM)] * 2,
        out_specs=[vmem] * len(parts),
        scratch_shapes=[
            pltpu.VMEM(source_channels.shape, jnp.int32), pltpu.VMEM(block.shape, jnp.bfloat16),
            pltpu.SemaphoreType.DMA(()), pltpu.SemaphoreType.DMA(()),
        ],
        compiler_params=pltpu.CompilerParams(vmem_limit_bytes=16 << 20),
    )(channel_counts, source_channels, block)
    one = [passed_along(piece, 1) for piece in own]
    other = [passed_along(piece, -1) for piece in own]
    table = make_table(bin_count, LAGS)
    table = jnp.concatenate([table[0], table[1]], axis=-1)
    def side(near, far, sums, index):
        last = index == len(parts) - 1
        return products(
            near[0], sources, chunk_of(table, index), own[index], near[index], far[index], sums, last, chips
        )

    given, kept = None, None
    for index in range(len(parts)):
        given = side(other, one, given, index)
        kept = side(one, other, kept, index)
        if index < len(parts) - 1:
            given, kept = lax.optimization_barrier((given, kept))
    taken = to_other_core(given)
    both = (kept.astype(jnp.float32) + taken.astype(jnp.float32)).astype(jnp.bfloat16)
    groups = [list(range(start, segments, 2)) for start in range(2)]
    received = lax.all_to_all(both, "seg", 0, 0, axis_index_groups=groups, tiled=True)
    summed = jnp.sum(received.astype(jnp.float32), axis=0)
    arrived = passed_along(summed, -1).reshape(2, 2, rows, -1)
    first_core = lax.axis_index("seg") % 2 == 0
    mine = jnp.where(first_core, arrived[:, 0], arrived[:, 1])
    theirs = to_other_core(jnp.where(first_core, arrived[:, 1], arrived[:, 0]))
    lower = jnp.where(first_core, theirs, mine)
    upper = jnp.where(first_core, mine, theirs)
    joined = jnp.concatenate([lower, upper[::-1]], axis=0)
    weights = pair_mask[0].astype(jnp.float32) * (1.0 / math.sqrt(segments))
    return (joined * weights[:, None, None])[None]


def solution(mesh):
    in_specs = (P("seg", "blk", None, None), P("blk", None), P("blk", None), P("blk"))
    out_specs = P("blk", None, "seg", None)
    return jax.shard_map(local, mesh=mesh, in_specs=in_specs, out_specs=out_specs, check_vma=False)
```
